256 devices in a mesh: dp: 2 (over x_hi), mx: 8 (over z), my: 16 (over x_lo, y, core).
Axes of the slice: x: 4 (x_hi: 2, x_lo: 2; x = x_hi * 2 + x_lo), y: 4, z: 8, core: 2. Of those that a mesh axis runs over, the one named last changes fastest.
Arguments:
- inputs: bfloat16 [2048, 6144], P(('dp', 'my'), 'mx'), may hold values from -6 to 6
- hidden_in: bfloat16 [2048, 24576], P(('dp', 'mx'), 'my'), may hold values from -6 to 6
- out_grad: bfloat16 [2048, 6144], P(('dp', 'my'), 'mx'), may hold values from -6 to 6
- up_weight: bfloat16 [6144, 24576], P('mx', 'my'), may hold values from -0.078125 to 0.078125
- down_weight: bfloat16 [24576, 6144], P('my', 'mx'), may hold values from -0.0390625 to 0.0390625
Outputs:
- inputs_grad: bfloat16 [2048, 6144], P(('dp', 'my'), 'mx')
- up_grad: bfloat16 [6144, 24576], P('mx', 'my')
- down_grad: bfloat16 [24576, 6144], P('my', 'mx')
The draws below stay inside these ranges and needn't reach their ends.
All inputs are finite; a program needn't handle non-finite values.
Results may differ from the reference program's by a relative error of at most 0.0059.
Values may be sent and summed in bfloat16 or wider, within the bound.
No kernel may reach another device: no remote copies, remote signals or barrier semaphores. Data moves between devices by JAX's collectives and lax.ppermute only.
A program may use at most 64 MiB of HBM per device.

```python
import jax
import jax.numpy as jnp
from jax import lax

D = 6144
FF = 24576
TOK_DEV = 1024
TOKENS = 2048
N_DP = 2


def shard_levels(key, shape, split, low, top_value):
    loudness, own = 1.0, jax.random.fold_in(key, 6)
    for dim, blocks in split:
        draws = jnp.exp(jax.random.uniform(jax.random.fold_in(own, dim), (blocks,), jnp.float32, low / len(split), top_value / len(split)))
        loudness = loudness * jnp.repeat(draws, shape[dim] // blocks).reshape([-1 if axis == dim else 1 for axis in range(len(shape))])
    return loudness


def gaussian(stream_key, dims, spread, reach, pieces=(), kind=jnp.bfloat16):
    entries = jax.random.normal(stream_key, dims, jnp.float32) * spread
    if len(pieces) > 0:
        entries = shard_levels(stream_key, dims, pieces, -0.22, 0.18) * entries
    return jnp.clip(entries, min=-reach, max=reach).astype(kind)


def setup_inputs(seed: int = 0) -> dict:
    key_of = jax.random.split(jax.random.key(seed), 6)
    inputs = gaussian(key_of[0], (TOKENS, D), 1.0, 6.0, ((0, 32), (1, 8)))
    hidden_in = gaussian(key_of[1], (TOKENS, FF), 1.5, 6.0, ((0, 16), (1, 16)))
    out_grad = gaussian(key_of[2], (TOKENS, D), 1.0, 6.0, ((0, 32), (1, 8)))
    up_weight = gaussian(key_of[3], (D, FF), D ** -0.5, 0.078125, ((0, 8), (1, 16)))
    down_weight = gaussian(key_of[4], (FF, D), FF ** -0.5, 0.0390625, ((0, 16), (1, 8)))
    return dict(inputs=inputs, hidden_in=hidden_in, out_grad=out_grad, up_weight=up_weight, down_weight=down_weight)


def gelu_value(value):
    return 0.5 * value * (1.0 + lax.erf(value * 0.7071067811865476))

def gelu_slope(value):
    return 0.5 * (1.0 + lax.erf(value * 0.7071067811865476)) + value * jnp.exp(-0.5 * value * value) * 0.3989422804014327

def reference(inputs, hidden_in, out_grad, up_weight, down_weight):
    pre_value = hidden_in.astype(jnp.float32)
    act = gelu_value(pre_value).astype(jnp.bfloat16)
    act_grad = jnp.dot(out_grad, down_weight.T, preferred_element_type=jnp.float32)
    pre_grad = (act_grad * gelu_slope(pre_value)).astype(jnp.bfloat16)
    inputs_grad = jnp.dot(pre_grad, up_weight.T, preferred_element_type=jnp.float32).astype(jnp.bfloat16)
    grad_scale = 1.0 / jnp.sqrt(jnp.float32(TOKENS))
    down_total = jnp.zeros((FF, D), jnp.float32)
    up_total = jnp.zeros((D, FF), jnp.float32)
    for half in range(N_DP):
        first_row = half * TOK_DEV
        act_block = act[first_row:first_row + TOK_DEV]
        grad_block = out_grad[first_row:first_row + TOK_DEV]
        input_block = inputs[first_row:first_row + TOK_DEV]
        pre_block = pre_grad[first_row:first_row + TOK_DEV]
        down_part = (jnp.dot(act_block.T, grad_block, preferred_element_type=jnp.float32) * grad_scale).astype(jnp.bfloat16)
        up_part = (jnp.dot(input_block.T, pre_block, preferred_element_type=jnp.float32) * grad_scale).astype(jnp.bfloat16)
        down_part = lax.optimization_barrier(down_part)
        up_part = lax.optimization_barrier(up_part)
        down_total = down_total + down_part.astype(jnp.float32)
        up_total = up_total + up_part.astype(jnp.float32)
    return (inputs_grad, up_total.astype(jnp.bfloat16), down_total.astype(jnp.bfloat16))
```

```python
import jax
import jax.numpy as jnp
from jax import lax
from jax.sharding import PartitionSpec as P


F32 = jnp.float32
BF16 = jnp.bfloat16
ALL = ("dp", "mx", "my")


def gelu_value(value):
    return 0.5 * value * (1.0 + lax.erf(value * 0.7071067811865476))


def gelu_slope(value):
    return (
        0.5 * (1.0 + lax.erf(value * 0.7071067811865476))
        + value * jnp.exp(-0.5 * value * value) * 0.3989422804014327
    )


def device_of(x, y, z, core):
    x, y, z, core = x % 4, y % 4, z % 8, core % 2
    return ((x // 2) * 8 + z) * 16 + ((x % 2) * 4 + y) * 2 + core


def shift(value, x=0, y=0, z=0, core=0):
    pairs = [
        (device_of(px, py, pz, pc), device_of(px + x, py + y, pz + z, pc + core))
        for px in range(4)
        for py in range(4)
        for pz in range(8)
        for pc in range(2)
    ]
    return lax.ppermute(value, ALL, pairs)


def put(whole, piece, *index):
    full = tuple(index) + (0,) * (whole.ndim - len(index))
    return lax.dynamic_update_slice(whole, piece, full)


def gather_plane(local, x, y, core):
    rows, cols = local.shape
    row = jnp.zeros((4, rows, cols), local.dtype)
    row = put(row, local[None], y)
    for step in (1, 3, 2):
        row = put(row, shift(local, y=step)[None], (y - step) % 4)
    plane = jnp.zeros((4, 4, rows, cols), local.dtype)
    plane = put(plane, row[None], x)
    for step in (1, 3, 2):
        plane = put(plane, shift(row, x=step)[None], (x - step) % 4)
    other = shift(plane, core=1)
    first = core == 0
    whole = jnp.stack(
        [jnp.where(first, plane, other), jnp.where(first, other, plane)], axis=2
    )
    return whole.reshape(16 * 2 * rows, cols)


def gather_z(local, z):
    rows, cols = local.shape
    half = cols // 2
    whole = jnp.zeros((2, 8, rows // 2, cols), local.dtype)

    def place(whole, piece, at, col=0):
        return lax.dynamic_update_slice(
            whole, piece.reshape(2, 1, rows // 2, piece.shape[1]), (0, at % 8, 0, col)
        )

    whole = place(whole, local, z)
    right = left = local
    for step in (1, 2, 3):
        right = shift(right, z=1)
        left = shift(left, z=-1)
        whole = place(whole, right, z - step)
        whole = place(whole, left, z + step)
    whole = place(whole, shift(right[:, :half], z=1), z - 4)
    whole = place(whole, shift(left[:, half:], z=-1), z + 4, half)
    return whole


def per_device(inputs, hidden_in, out_grad, up_weight, down_weight):
    dp, z, my = lax.axis_index("dp"), lax.axis_index("mx"), lax.axis_index("my")
    x, y, core = dp * 2 + my // 8, (my // 2) % 4, my % 2
    tokens = out_grad.shape[0] * lax.axis_size("my") * lax.axis_size("dp")
    grad_scale = 1.0 / jnp.sqrt(jnp.float32(tokens))
    part = hidden_in.shape[1] // 2

    def dot(a, b, dims):
        return lax.dot_general(a, b, (dims, ((), ())), preferred_element_type=F32)

    mine = lax.dynamic_slice_in_dim(hidden_in, dp * part, part, 1)
    theirs = lax.dynamic_slice_in_dim(hidden_in, (1 - dp) * part, part, 1)
    came = shift(theirs, x=2)
    first = dp == 0
    hidden = jnp.concatenate(
        [jnp.where(first, mine, came), jnp.where(first, came, mine)], axis=0
    ).astype(F32)
    act = gelu_value(hidden).astype(BF16)
    slope = gelu_slope(hidden)

    down_half = lax.dynamic_slice_in_dim(down_weight, dp * part, part, 0)
    up_half = lax.dynamic_slice_in_dim(up_weight, dp * part, part, 1)

    grad_whole = gather_plane(out_grad, x, y, core)
    act_whole = gather_z(act, z)

    grad_chunks = grad_whole.reshape(2, 8, 128, -1)
    half = part // 2

    def partial(at):
        rows = lax.dynamic_slice_in_dim(grad_chunks, at % 8, 1, 1).reshape(256, -1)
        return dot(rows, down_half, ((1,), (1,)))

    far = partial(z + 4).astype(BF16)
    right = shift(far[:, :half], z=1).astype(F32)
    left = shift(far[:, half:], z=-1).astype(F32)
    right = jnp.pad(right, ((0, 0), (0, half)))
    left = jnp.pad(left, ((0, 0), (half, 0)))
    for step in (3, 2, 1):
        right = shift((partial(z + step) + right).astype(BF16), z=1).astype(F32)
        left = shift((partial(z - step) + left).astype(BF16), z=-1).astype(F32)
    act_grad = partial(z) + right + left
    pre = (act_grad * slope).astype(BF16)

    input_whole = gather_plane(inputs, x, y, core)
    act_rows = act_whole.reshape(2048, part)
    down_mine = (dot(act_rows, grad_whole, ((0,), (0,))) * grad_scale).astype(BF16)
    down_theirs = shift(down_mine, x=2)

    pre_rows = gather_z(pre, z).reshape(2048, part)
    up_mine = (dot(input_whole, pre_rows, ((0,), (0,))) * grad_scale).astype(BF16)
    up_theirs = shift(up_mine, x=2)

    total = dot(pre_rows, up_half, ((1,), (1,))).reshape(4, 4, 2, 64, -1)

    def pick(value, at, axis):
        return lax.dynamic_index_in_dim(value, at, axis, keepdims=False)

    total = pick(total, core, 2) + shift(pick(total, 1 - core, 2).astype(BF16), core=1).astype(F32)
    narrow = total.astype(BF16)
    total = pick(total, y, 1)
    for step in (1, 3, 2):
        total = total + shift(pick(narrow, (y + step) % 4, 1), y=step).astype(F32)
    narrow = total.astype(BF16)
    total = pick(total, x, 0)
    for step in (1, 3, 2):
        total = total + shift(pick(narrow, (x + step) % 4, 0), x=step).astype(F32)

    up_grad = jnp.concatenate(
        [jnp.where(first, up_mine, up_theirs), jnp.where(first, up_theirs, up_mine)], axis=1
    )
    down_grad = jnp.concatenate(
        [jnp.where(first, down_mine, down_theirs), jnp.where(first, down_theirs, down_mine)], axis=0
    )
    return total.astype(BF16), up_grad, down_grad


def solution(mesh):
    return jax.shard_map(
        per_device,
        mesh=mesh,
        in_specs=(
            P(("dp", "my"), "mx"),
            P(("dp", "mx"), "my"),
            P(("dp", "my"), "mx"),
            P("mx", "my"),
            P("my", "mx"),
        ),
        out_specs=(P(("dp", "my"), "mx"), P("mx", "my"), P("my", "mx")),
        check_vma=False,
    )
```

```python
import jax
import jax.numpy as jnp
from jax import lax
from jax.sharding import PartitionSpec as P


F32 = jnp.float32
BF16 = jnp.bfloat16
ALL = ("dp", "mx", "my")


def gelu_value(value):
    return 0.5 * value * (1.0 + lax.erf(value * 0.7071067811865476))


def gelu_slope(value):
    return (
        0.5 * (1.0 + lax.erf(value * 0.7071067811865476))
        + value * jnp.exp(-0.5 * value * value) * 0.3989422804014327
    )


def device_of(x, y, z, core):
    return ((x // 2) * 8 + z % 8) * 16 + ((x % 2) * 4 + y) * 2 + core


def shift(value, x=0, y=0, core=0, z=None):
    def over(pz):
        return pz if z is None else pz + (1 if (pz % 2 == 0) == (z == "e") else -1)

    pairs = [
        (device_of(px, py, pz, pc), device_of(px ^ x, py ^ y, over(pz), pc ^ core))
        for px in range(4)
        for py in range(4)
        for pz in range(8)
        for pc in range(2)
    ]
    return lax.ppermute(value, ALL, pairs)


OTHER = {"e": "o", "o": "e"}


def link(chain, step):
    return chain if step % 2 == 1 else OTHER[chain]


def dot(a, b, dims):
    return lax.dot_general(a, b, (dims, ((), ())), preferred_element_type=F32)


def gather_x_y(local):
    row = jnp.stack([local] + [shift(local, x=k) for k in (1, 2, 3)], 0)
    return [row] + [shift(row, y=k) for k in (1, 2, 3)]


def gather_core(rows):
    plane = jnp.stack(rows, 1).reshape(2, 8, 64, -1)
    return jnp.stack([plane, shift(plane, core=1)], 0)


def per_device(inputs, hidden_in, out_grad, up_weight, down_weight):
    dp, z, my = lax.axis_index("dp"), lax.axis_index("mx"), lax.axis_index("my")
    own, core = my // 2, my % 2
    tokens = out_grad.shape[0] * lax.axis_size("my") * lax.axis_size("dp")
    grad_scale = 1.0 / jnp.sqrt(jnp.float32(tokens))
    part = hidden_in.shape[1] // 2
    half = part // 2

    even = 1 - 2 * (z % 2)

    def slot(chain, step):
        away = step * (1 if step % 2 == 1 else -1) * (1 if chain == "e" else -1) * even
        return lax.bitwise_xor(lax.rem(z + away + 8, 8), own)

    def by_core(rows):
        rows = rows.reshape(2, 64, part)
        return jnp.where(core == 0, rows, rows[::-1])

    mine = by_core(lax.dynamic_slice_in_dim(hidden_in, dp * part, part, 1))
    theirs = by_core(lax.dynamic_slice_in_dim(hidden_in, (1 - dp) * part, part, 1))
    hidden = (mine, shift(theirs, x=2))
    hidden = jnp.stack(hidden, 1).astype(F32)
    act = gelu_value(hidden).astype(BF16)
    act, slope = lax.optimization_barrier((act, gelu_slope(hidden)))

    down_half = lax.dynamic_slice_in_dim(down_weight, dp * part, part, 0)
    up_half = lax.dynamic_slice_in_dim(up_weight, dp * part, part, 1)

    grad_whole = gather_core(gather_x_y(out_grad))
    input_rows = gather_x_y(inputs)

    def spread(piece, split, before=None):
        cols = piece.shape[-1]
        whole = jnp.zeros((2, 2, 8, 64, cols), BF16)

        def place(whole, piece, at, col=0):
            return lax.dynamic_update_slice(whole, piece[:, :, None], (0, 0, at, 0, col))

        whole = place(whole, piece, slot("e", 0))
        came = {"e": piece, "o": piece}
        for step in (1, 2, 3):
            for chain in "eo":
                came[chain] = shift(came[chain], z=link(chain, step))
                whole = place(whole, came[chain], slot(chain, step))
        far = []
        if split > 0:
            far.append((shift(came["e"][..., :split], z="o"), 0))
        if split < cols:
            far.append((shift(came["o"][..., split:], z="e"), split))
        if before is not None:
            pieces = lax.optimization_barrier(([piece for piece, _ in far], before))[0]
            far = [(piece, col) for piece, (_, col) in zip(pieces, far)]
        for piece, col in far:
            whole = place(whole, piece, slot("e", 4), col)
        return whole.reshape(2048, cols)

    act_whole = spread(act, half)

    sums = dot(grad_whole.reshape(2048, -1), down_half, ((1,), (1,))).reshape(2, 2, 8, 64, part)

    def term(chain, step):
        return lax.dynamic_index_in_dim(sums, slot(chain, step), 2, keepdims=False)

    far = lax.dynamic_index_in_dim(grad_whole, slot("e", 4), 2, keepdims=False).reshape(256, -1)
    far = dot(far, down_half, ((1,), (1,))).astype(BF16).reshape(2, 2, 64, part)
    blank = [jnp.zeros(up_weight.shape, BF16), jnp.zeros(down_weight.shape, BF16)]
    pad = ((0, 0), (0, 0), (0, 0))
    came = {
        "e": jnp.pad(shift(far[..., :half], z="o").astype(F32), pad + ((0, half),)),
        "o": jnp.pad(shift(far[..., half:], z="e").astype(F32), pad + ((half, 0),)),
    }
    for step in (3, 2, 1):
        send = [(term(chain, step) + came[chain]).astype(BF16) for chain in "eo"]
        if step == 1:
            send, input_rows = lax.optimization_barrier((send, input_rows))
        elif step == 2:
            send, blank = lax.optimization_barrier((send, blank))
        else:
            send = lax.optimization_barrier(send)
        came = {chain: shift(value, z=link(chain, step)).astype(F32) for chain, value in zip("eo", send)}
    pre = ((term("e", 0) + came["e"] + came["o"]) * slope).astype(BF16)
    input_whole = gather_core(input_rows).reshape(2048, -1)

    first = dp * part
    grad_rows = grad_whole.reshape(2048, -1)
    down_mine = (dot(act_whole, grad_rows, ((0,), (0,))) * grad_scale).astype(BF16)
    down_mine = lax.optimization_barrier(down_mine)
    down_grad = lax.dynamic_update_slice(blank[1], down_mine, (first, 0))
    down_grad = lax.dynamic_update_slice(down_grad, shift(down_mine, x=2), (part - first, 0))

    up_mine, up_theirs, rows, total = [], [], [], None
    for col, split in ((0, half), (half, 0)):
        rows.append(spread(pre[..., col:col + half], split, up_mine or None))
        block = (dot(input_whole, rows[-1], ((0,), (0,))) * grad_scale).astype(BF16)
        up_mine.append(lax.optimization_barrier(block))
        up_theirs.append(shift(up_mine[-1], x=2))
        if total is None:
            total = dot(rows[0], up_half[:, :half], ((1,), (1,)))
            total, up_mine[0] = lax.optimization_barrier((total, up_mine[0]))

    up_grad = blank[0]
    for k in (0, 1):
        up_grad = lax.dynamic_update_slice(up_grad, up_mine[k], (0, first + k * half))
    for k in (0, 1):
        up_grad = lax.dynamic_update_slice(up_grad, up_theirs[k], (0, part - first + k * half))


    def rest(side):
        side = slice(side * 1024, side * 1024 + 1024)
        return total[side] + dot(rows[1][side], up_half[:, half:], ((1,), (1,)))

    came = shift(rest(1).astype(BF16), core=1)
    total = (rest(0) + came.astype(F32)).reshape(4, 4, 64, -1)
    narrow = total.astype(BF16)
    total = total[:, 0]
    for k in (1, 3, 2):
        total = total + shift(narrow[:, k], y=k).astype(F32)
    narrow = total.astype(BF16)
    total = total[0]
    for k in (1, 3, 2):
        total = total + shift(narrow[k], x=k).astype(F32)
    return total.astype(BF16), up_grad, down_grad


def solution(mesh):
    return jax.shard_map(
        per_device,
        mesh=mesh,
        in_specs=(
            P(("dp", "my"), "mx"),
            P(("dp", "mx"), "my"),
            P(("dp", "my"), "mx"),
            P("mx", "my"),
            P("my", "mx"),
        ),
        out_specs=(P(("dp", "my"), "mx"), P("mx", "my"), P("my", "mx")),
        check_vma=False,
    )
```

```python
import jax
import jax.numpy as jnp
from jax import lax
from jax.sharding import PartitionSpec as P


F32 = jnp.float32
BF16 = jnp.bfloat16
ALL = ("dp", "mx", "my")


def gelu_value(value):
    return 0.5 * value * (1.0 + lax.erf(value * 0.7071067811865476))


def gelu_slope(value):
    return (
        0.5 * (1.0 + lax.erf(value * 0.7071067811865476))
        + value * jnp.exp(-0.5 * value * value) * 0.3989422804014327
    )


def device_of(x, y, z, core):
    return ((x // 2) * 8 + z % 8) * 16 + ((x % 2) * 4 + y) * 2 + core


def shift(value, x=0, y=0, core=0, z=None):
    def over(pz):
        return pz if z is None else pz + (1 if (pz % 2 == 0) == (z == "e") else -1)

    pairs = [
        (device_of(px, py, pz, pc), device_of(px ^ x, py ^ y, over(pz), pc ^ core))
        for px in range(4)
        for py in range(4)
        for pz in range(8)
        for pc in range(2)
    ]
    return lax.ppermute(value, ALL, pairs)


OTHER = {"e": "o", "o": "e"}


def link(chain, step):
    return chain if step % 2 == 1 else OTHER[chain]


def dot(a, b, dims):
    return lax.dot_general(a, b, (dims, ((), ())), preferred_element_type=F32)


def gather_x_y(local):
    row = jnp.stack([local] + [shift(local, x=k) for k in (1, 2, 3)], 0)
    return [row] + [shift(row, y=k) for k in (1, 2, 3)]


def gather_core(rows):
    plane = jnp.stack(rows, 1).reshape(2, 8, 64, -1)
    other = shift(plane, core=1)
    return jnp.stack([plane, other], 0)


def per_device(inputs, hidden_in, out_grad, up_weight, down_weight):
    dp, z, my = lax.axis_index("dp"), lax.axis_index("mx"), lax.axis_index("my")
    own, core = my // 2, my % 2
    tokens = out_grad.shape[0] * lax.axis_size("my") * lax.axis_size("dp")
    grad_scale = 1.0 / jnp.sqrt(jnp.float32(tokens))
    part = hidden_in.shape[1] // 2
    half = part // 2

    even = 1 - 2 * (z % 2)

    def slot(chain, step):
        away = step * (1 if step % 2 == 1 else -1) * (1 if chain == "e" else -1) * even
        return lax.bitwise_xor(lax.rem(z + away + 8, 8), own)

    def by_core(rows):
        rows = rows.reshape(2, 64, part)
        return jnp.where(core == 0, rows, rows[::-1])

    mine = by_core(lax.dynamic_slice_in_dim(hidden_in, dp * part, part, 1))
    theirs = by_core(lax.dynamic_slice_in_dim(hidden_in, (1 - dp) * part, part, 1))
    hidden = (mine, shift(theirs, x=2))
    hidden = jnp.stack(hidden, 1).astype(F32)
    act = gelu_value(hidden).astype(BF16)
    act, slope = lax.optimization_barrier((act, gelu_slope(hidden)))

    down_half = lax.dynamic_slice_in_dim(down_weight, dp * part, part, 0)
    up_half = lax.dynamic_slice_in_dim(up_weight, dp * part, part, 1)

    grad_whole = gather_core(gather_x_y(out_grad))
    input_rows = gather_x_y(inputs)

    def spread(piece, split, before=None):
        cols = piece.shape[-1]
        whole = jnp.zeros((2, 2, 8, 64, cols), BF16)

        def place(whole, piece, at, col=0):
            return lax.dynamic_update_slice(whole, piece[:, :, None], (0, 0, at, 0, col))

        whole = place(whole, piece, slot("e", 0))
        came = {"e": piece, "o": piece}
        for step in (1, 2, 3):
            for chain in "eo":
                came[chain] = shift(came[chain], z=link(chain, step))
                whole = place(whole, came[chain], slot(chain, step))
        far = []
        if split > 0:
            far.append((shift(came["e"][..., :split], z="o"), 0))
        if split < cols:
            far.append((shift(came["o"][..., split:], z="e"), split))
        if before is not None:
            pieces = lax.optimization_barrier(([piece for piece, _ in far], before))
            pieces, before = pieces
            far = [(piece, col) for piece, (_, col) in zip(pieces, far)]
        for piece, col in far:
            whole = place(whole, piece, slot("e", 4), col)
        return whole.reshape(2048, cols), before

    act_whole, _ = spread(act, half)

    sums = dot(grad_whole.reshape(2048, -1), down_half, ((1,), (1,)))
    sums = sums.reshape(2, 2, 8, 64, part)

    def term(chain, step):
        return lax.dynamic_index_in_dim(sums, slot(chain, step), 2, keepdims=False)

    far = lax.dynamic_index_in_dim(grad_whole, slot("e", 4), 2, keepdims=False).reshape(256, -1)
    far = dot(far, down_half, ((1,), (1,))).astype(BF16).reshape(2, 2, 64, part)
    blank = [jnp.zeros(up_weight.shape, BF16), jnp.zeros(down_weight.shape, BF16)]
    pad = ((0, 0), (0, 0), (0, 0))
    came = {
        "e": jnp.pad(shift(far[..., :half], z="o").astype(F32), pad + ((0, half),)),
        "o": jnp.pad(shift(far[..., half:], z="e").astype(F32), pad + ((half, 0),)),
    }
    for step in (3, 2, 1):
        send = [(term(chain, step) + came[chain]).astype(BF16) for chain in "eo"]
        if step == 2:
            send, blank = lax.optimization_barrier((send, blank))
        else:
            send = lax.optimization_barrier(send)
        came = {
            chain: shift(value, z=link(chain, step)).astype(F32)
            for chain, value in zip("eo", send)
        }
    pre = ((term("e", 0) + came["e"] + came["o"]) * slope).astype(BF16)
    input_whole = gather_core(input_rows).reshape(2048, -1)

    first = dp * part
    grad_rows = grad_whole.reshape(2048, -1)
    down_mine = (dot(act_whole, grad_rows, ((0,), (0,))) * grad_scale).astype(BF16)
    down_mine = lax.optimization_barrier(down_mine)
    down_theirs = shift(down_mine, x=2)
    down_grad = lax.dynamic_update_slice(blank[1], down_mine, (first, 0))
    down_grad = lax.dynamic_update_slice(down_grad, down_theirs, (part - first, 0))

    up_mine, up_theirs, rows = [], [], []
    for col, split in ((0, half), (half, 0)):
        whole, before = spread(pre[..., col:col + half], split, up_mine or None)
        if before:
            up_mine = list(before)
        rows.append(whole)
        block = (dot(input_whole, rows[-1], ((0,), (0,))) * grad_scale).astype(BF16)
        up_mine.append(lax.optimization_barrier(block))
        up_theirs.append(shift(up_mine[-1], x=2))

    up_grad = blank[0]
    for k in (0, 1):
        up_grad = lax.dynamic_update_slice(up_grad, up_mine[k], (0, first + k * half))
    for k in (0, 1):
        up_grad = lax.dynamic_update_slice(up_grad, up_theirs[k], (0, part - first + k * half))


    def rest(side):
        side = slice(side * 1024, side * 1024 + 1024)
        return dot(jnp.concatenate([part_rows[side] for part_rows in rows], 1), up_half, ((1,), (1,)))

    came = shift(rest(1).astype(BF16), core=1)
    total = (rest(0) + came.astype(F32)).reshape(4, 4, 64, -1)
    narrow = total.astype(BF16)
    total = total[:, 0]
    for k in (1, 3, 2):
        total = total + shift(narrow[:, k], y=k).astype(F32)
    narrow = total.astype(BF16)
    total = total[0]
    for k in (1, 3, 2):
        total = total + shift(narrow[k], x=k).astype(F32)
    return total.astype(BF16), up_grad, down_grad


def solution(mesh):
    return jax.shard_map(
        per_device,
        mesh=mesh,
        in_specs=(
            P(("dp", "my"), "mx"),
            P(("dp", "mx"), "my"),
            P(("dp", "my"), "mx"),
            P("mx", "my"),
            P("my", "mx"),
        ),
        out_specs=(P(("dp", "my"), "mx"), P("mx", "my"), P("my", "mx")),
        check_vma=False,
    )
```

```python
import jax
import jax.numpy as jnp
from jax import lax
from jax.sharding import PartitionSpec as P


F32 = jnp.float32
BF16 = jnp.bfloat16
ALL = ("dp", "mx", "my")


def gelu_value(value):
    return 0.5 * value * (1.0 + lax.erf(value * 0.7071067811865476))


def gelu_slope(value):
    return (
        0.5 * (1.0 + lax.erf(value * 0.7071067811865476))
        + value * jnp.exp(-0.5 * value * value) * 0.3989422804014327
    )


def device_of(x, y, z, core):
    return ((x // 2) * 8 + z % 8) * 16 + ((x % 2) * 4 + y) * 2 + core


def shift(value, x=0, y=0, core=0, z=None):
    def over(pz):
        return pz if z is None else pz + (1 if (pz % 2 == 0) == (z == "e") else -1)

    pairs = [
        (device_of(px, py, pz, pc), device_of(px ^ x, py ^ y, over(pz), pc ^ core))
        for px in range(4)
        for py in range(4)
        for pz in range(8)
        for pc in range(2)
    ]
    return lax.ppermute(value, ALL, pairs)


OTHER = {"e": "o", "o": "e"}


def link(chain, step):
    return chain if step % 2 == 1 else OTHER[chain]


def dot(a, b, dims):
    return lax.dot_general(a, b, (dims, ((), ())), preferred_element_type=F32)


def gather_x_y(local):
    row = jnp.stack([local] + [shift(local, x=k) for k in (1, 2, 3)], 0)
    return [row] + [shift(row, y=k) for k in (1, 2, 3)]


def gather_core(rows):
    plane = jnp.stack(rows, 1).reshape(2, 8, 64, -1)
    other = shift(plane, core=1)
    return jnp.stack([plane, other], 0)


def per_device(inputs, hidden_in, out_grad, up_weight, down_weight):
    dp, z, my = lax.axis_index("dp"), lax.axis_index("mx"), lax.axis_index("my")
    own, core = my // 2, my % 2
    tokens = out_grad.shape[0] * lax.axis_size("my") * lax.axis_size("dp")
    grad_scale = 1.0 / jnp.sqrt(jnp.float32(tokens))
    part = hidden_in.shape[1] // 2
    half = part // 2

    even = 1 - 2 * (z % 2)

    def slot(chain, step):
        away = step * (1 if step % 2 == 1 else -1) * (1 if chain == "e" else -1) * even
        return lax.bitwise_xor(lax.rem(z + away + 8, 8), own)

    def by_core(rows):
        rows = rows.reshape(2, 64, part)
        return jnp.where(core == 0, rows, rows[::-1])

    mine = by_core(lax.dynamic_slice_in_dim(hidden_in, dp * part, part, 1))
    theirs = by_core(lax.dynamic_slice_in_dim(hidden_in, (1 - dp) * part, part, 1))
    hidden = (mine, shift(theirs, x=2))
    hidden = jnp.stack(hidden, 1).astype(F32)
    act = gelu_value(hidden).astype(BF16)
    act, slope = lax.optimization_barrier((act, gelu_slope(hidden)))

    down_half = lax.dynamic_slice_in_dim(down_weight, dp * part, part, 0)
    up_half = lax.dynamic_slice_in_dim(up_weight, dp * part, part, 1)

    grad_whole = gather_core(gather_x_y(out_grad))
    input_rows = gather_x_y(inputs)

    def spread(piece, split, before=None):
        cols = piece.shape[-1]
        whole = jnp.zeros((2, 2, 8, 64, cols), BF16)

        def place(whole, piece, at, col=0):
            return lax.dynamic_update_slice(whole, piece[:, :, None], (0, 0, at, 0, col))

        whole = place(whole, piece, slot("e", 0))
        came = {"e": piece, "o": piece}
        for step in (1, 2, 3):
            for chain in "eo":
                came[chain] = shift(came[chain], z=link(chain, step))
                whole = place(whole, came[chain], slot(chain, step))
        far = []
        if split > 0:
            far.append((shift(came["e"][..., :split], z="o"), 0))
        if split < cols:
            far.append((shift(came["o"][..., split:], z="e"), split))
        if before is not None:
            pieces = lax.optimization_barrier(([piece for piece, _ in far], before))
            pieces, before = pieces
            far = [(piece, col) for piece, (_, col) in zip(pieces, far)]
        for piece, col in far:
            whole = place(whole, piece, slot("e", 4), col)
        return whole.reshape(2048, cols), before

    act_whole, _ = spread(act, half)

    sums = dot(grad_whole.reshape(2048, -1), down_half, ((1,), (1,)))
    sums = sums.reshape(2, 2, 8, 64, part)

    def term(chain, step):
        return lax.dynamic_index_in_dim(sums, slot(chain, step), 2, keepdims=False)

    far = lax.dynamic_index_in_dim(grad_whole, slot("e", 4), 2, keepdims=False).reshape(256, -1)
    far = dot(far, down_half, ((1,), (1,))).astype(BF16).reshape(2, 2, 64, part)
    blank = [jnp.zeros(up_weight.shape, BF16), jnp.zeros(down_weight.shape, BF16)]
    pad = ((0, 0), (0, 0), (0, 0))
    came = {
        "e": jnp.pad(shift(far[..., :half], z="o").astype(F32), pad + ((0, half),)),
        "o": jnp.pad(shift(far[..., half:], z="e").astype(F32), pad + ((half, 0),)),
    }
    for step in (3, 2, 1):
        send = [(term(chain, step) + came[chain]).astype(BF16) for chain in "eo"]
        if step == 2:
            send, blank = lax.optimization_barrier((send, blank))
        else:
            send = lax.optimization_barrier(send)
        came = {chain: shift(value, z=link(chain, step)).astype(F32) for chain, value in zip("eo", send)}
    pre = ((term("e", 0) + came["e"] + came["o"]) * slope).astype(BF16)
    input_whole = gather_core(input_rows).reshape(2048, -1)

    first = dp * part
    grad_rows = grad_whole.reshape(2048, -1)
    down_mine = (dot(act_whole, grad_rows, ((0,), (0,))) * grad_scale).astype(BF16)
    down_mine = lax.optimization_barrier(down_mine)
    down_theirs = shift(down_mine, x=2)
    down_grad = lax.dynamic_update_slice(blank[1], down_mine, (first, 0))
    down_grad = lax.dynamic_update_slice(down_grad, down_theirs, (part - first, 0))

    up_mine, up_theirs, rows = [], [], []
    for col, split in ((0, half), (half, 0)):
        whole, before = spread(pre[..., col:col + half], split, up_mine or None)
        if before:
            up_mine = list(before)
        rows.append(whole)
        block = (dot(input_whole, rows[-1], ((0,), (0,))) * grad_scale).astype(BF16)
        up_mine.append(lax.optimization_barrier(block))
        up_theirs.append(shift(up_mine[-1], x=2))

    up_grad = blank[0]
    for k in (0, 1):
        up_grad = lax.dynamic_update_slice(up_grad, up_mine[k], (0, first + k * half))
    for k in (0, 1):
        up_grad = lax.dynamic_update_slice(up_grad, up_theirs[k], (0, part - first + k * half))


    def rest(side):
        side = slice(side * 1024, side * 1024 + 1024)
        return dot(jnp.concatenate([part_rows[side] for part_rows in rows], 1), up_half, ((1,), (1,)))

    came = shift(rest(1).astype(BF16), core=1)
    total = (lax.optimization_barrier(rest(0)) + came.astype(F32)).reshape(4, 4, 64, -1)
    narrow = total.astype(BF16)
    total = total[:, 0]
    for k in (1, 3, 2):
        total = total + shift(narrow[:, k], y=k).astype(F32)
    narrow = total.astype(BF16)
    total = total[0]
    for k in (1, 3, 2):
        total = total + shift(narrow[k], x=k).astype(F32)
    return total.astype(BF16), up_grad, down_grad


def solution(mesh):
    return jax.shard_map(
        per_device,
        mesh=mesh,
        in_specs=(
            P(("dp", "my"), "mx"),
            P(("dp", "mx"), "my"),
            P(("dp", "my"), "mx"),
            P("mx", "my"),
            P("my", "mx"),
        ),
        out_specs=(P(("dp", "my"), "mx"), P("mx", "my"), P("my", "mx")),
        check_vma=False,
    )
```
